32 devices in a mesh: chan: 8 (over z, x), tm: 4 (over y, core).
Axes of the slice: x: 2, y: 2, z: 4, core: 2. Of those that a mesh axis runs over, the one named last changes fastest.
Arguments:
- samples: bfloat16 [2048, 131072], P('chan', 'tm'), may hold values from -6 to 6
- fir_taps: float32 [8, 4096], replicated, may hold values from -2 to 2
- beam_y: bfloat16 [2, 32, 32], replicated, may hold values from -0.75 to 0.75
- beam_x: bfloat16 [2, 64, 64], replicated, may hold values from -0.5 to 0.5
- delays: int32 [64, 2048], replicated, may hold values from 0 to 8, as said below
Outputs:
- series: float32 [2048, 32, 64], P('chan', 'tm')
The draws below stay inside these ranges and needn't reach their ends.
Inputs may be any that keep to these rules, and one draw needn't show every extreme that they name: Each trial's delays come from a dispersion law: along a row they never rise with the channel index; the largest value is reached.
All inputs are finite; a program needn't handle non-finite values.
Results may differ from the reference program's by a relative error of at most 0.00068.
Values may be sent and summed in bfloat16 or wider, within the bound.
No kernel may reach another device: no remote copies, remote signals or barrier semaphores. Data moves between devices by JAX's collectives and lax.ppermute only.
A program may use at most 192 MiB of HBM per device.

```python
import math
import jax
import jax.numpy as jnp
from jax import lax

NFFT = 4096
TAPS = 8
DX = 64
DY = 32
TRIALS = 64
SPEC_DEV = 8
CH = 2048
DISH = 2048
BEAMS = 2048
WINDOW = 32


def draw_delays(key, part):
    key_measure = jax.random.fold_in(key, 11)
    key_pick = jax.random.fold_in(key, 23)
    measure = jax.random.randint(key_measure, (TRIALS,), 0, 1001, dtype=jnp.int32)
    chosen = jax.random.randint(key_pick, (), 0, TRIALS, dtype=jnp.int32)
    measure = jnp.where(jnp.arange(TRIALS, dtype=jnp.int32) == chosen, 1000, measure)
    channel = jnp.arange(CH, dtype=jnp.int32)
    curve = 400 * CH * CH // ((CH + channel) * (CH + channel)) - 100
    return measure[:, None] * curve[None, :] * SPEC_DEV // 300000


def block_scale(own_key, extent, cuts, low, high):
    gain, own = 1.0, jax.random.fold_in(own_key, 6)
    for dim, parts in cuts:
        heights = jnp.exp(jax.random.uniform(jax.random.fold_in(own, dim), (parts,), jnp.float32, low / len(cuts), high / len(cuts)))
        gain = gain * jnp.repeat(heights, extent[dim] // parts).reshape([-1 if axis == dim else 1 for axis in range(len(extent))])
    return gain


def noise(key, dims, scale, most, pieces=(), kind=jnp.bfloat16):
    loudness = block_scale(key, dims, pieces, -0.22, 0.18) if pieces else 1.0
    values = jax.random.normal(key, dims, jnp.float32) * scale * loudness
    return jnp.minimum(jnp.maximum(values, -most), most).astype(kind)


def setup_inputs(seed: int = 0) -> dict:
    seeds = jax.random.split(jax.random.key(seed), 6)
    samples = noise(seeds[0], (DISH, WINDOW * NFFT), 1.0, 6.0, ((0, 8), (1, 4)))
    fir_taps = noise(seeds[1], (TAPS, NFFT), TAPS ** -0.5, 2.0, (), jnp.float32)
    beam_y = noise(seeds[2], (2, DY, DY), (2 * DY) ** -0.5, 0.75)
    beam_x = noise(seeds[3], (2, DX, DX), (2 * DX) ** -0.5, 0.5)
    delays = draw_delays(jax.random.fold_in(seeds[5], 71), 0)
    return dict(samples=samples, fir_taps=fir_taps, beam_y=beam_y, beam_x=beam_x, delays=delays)


def complex_apply(weights, real_part, imag_part, form):
    w_real = weights[0].astype(jnp.float32)
    w_imag = weights[1].astype(jnp.float32)
    out_real = jnp.einsum(form, w_real, real_part) - jnp.einsum(form, w_imag, imag_part)
    out_imag = jnp.einsum(form, w_real, imag_part) + jnp.einsum(form, w_imag, real_part)
    return (out_real, out_imag)

def rounded(value):
    kept = lax.optimization_barrier(value.astype(jnp.bfloat16))
    return kept.astype(jnp.float32)

def reference(samples, fir_taps, beam_y, beam_x, delays):
    frames = samples.reshape(DISH, WINDOW, NFFT)
    padded = jnp.concatenate([jnp.zeros((DISH, TAPS - 1, NFFT), samples.dtype), frames], axis=1)
    reversed_taps = fir_taps[::-1].astype(jnp.float32)

    def one_spectrum(position):
        block = lax.dynamic_slice_in_dim(padded, position.astype(jnp.int32), TAPS, 1).astype(jnp.float32)
        filtered = lax.optimization_barrier(jnp.sum(block * reversed_taps[None], axis=1))
        spectrum = jnp.fft.fft(filtered, axis=-1)[:, :CH] * (1.0 / math.sqrt(NFFT))
        volt_real = rounded(jnp.real(spectrum)).reshape(DX, DY, CH)
        volt_imag = rounded(jnp.imag(spectrum)).reshape(DX, DY, CH)
        part_real, part_imag = complex_apply(beam_y, volt_real, volt_imag, 'py,xyc->xpc')
        part_real = rounded(part_real)
        part_imag = rounded(part_imag)
        form_real, form_imag = complex_apply(beam_x, part_real, part_imag, 'qx,xpc->qpc')
        power = (form_real * form_real + form_imag * form_imag).reshape(BEAMS, CH)
        return (power - lax.optimization_barrier(jnp.mean(power, axis=0, keepdims=True))).astype(jnp.bfloat16)
    powers = lax.map(one_spectrum, jnp.arange(WINDOW, dtype=jnp.int32))
    block_beams = min(256, BEAMS)
    powers = jnp.concatenate([powers, jnp.zeros((SPEC_DEV, BEAMS, CH), powers.dtype)], axis=0)
    blocks = jnp.moveaxis(powers.reshape(WINDOW + SPEC_DEV, BEAMS // block_beams, block_beams, CH), 1, 0)

    def one_block(block):

        def turn(shift_value, total):
            piece = lax.dynamic_slice_in_dim(block, shift_value.astype(jnp.int32), WINDOW, 0).astype(jnp.float32)
            selector = (delays == shift_value.astype(jnp.int32)).astype(jnp.float32)
            return total + jnp.einsum('sbc,tc->bst', piece, selector)
        return lax.fori_loop(0, SPEC_DEV + 1, turn, jnp.zeros((block_beams, WINDOW, TRIALS), jnp.float32))
    series = lax.map(one_block, blocks).reshape(BEAMS, WINDOW, TRIALS)
    return series * (1.0 / math.sqrt(CH))
```

```python
import functools
import math

import jax
import jax.numpy as jnp
import numpy as np
from jax import lax
from jax.experimental import pallas as pl
from jax.experimental.pallas import tpu as pltpu
from jax.sharding import PartitionSpec as P


LANES = 128
GROUP_X = 4
PAIR = 2
BF16 = jnp.bfloat16
F32 = jnp.float32


def shifted(array, axis, by):
    count = lax.axis_size(axis)
    pairs = [(i, i + by) for i in range(count) if 0 <= i + by < count]
    return lax.ppermute(array, axis, pairs)


def phase_table(rows_count, cols_count, period):
    row_index = jnp.arange(rows_count, dtype=jnp.int32)[:, None]
    col_index = jnp.arange(cols_count, dtype=jnp.int32)[None, :]
    angle = (row_index * col_index % period).astype(jnp.float32) * (2.0 * math.pi / period)
    return (jnp.cos(angle), jnp.sin(angle))


def transform(frames_rows, nfft):
    bits = nfft.bit_length() - 1
    first = 1 << bits // 2
    second = nfft // first
    rows_count = frames_rows.shape[0]
    shaped = frames_rows.reshape(rows_count, first, second)
    highest = lax.Precision.HIGHEST
    cos_one, sin_one = phase_table(first, first, first)
    section_real = jnp.einsum("rab,ak->rkb", shaped, cos_one, precision=highest)
    section_imag = -jnp.einsum("rab,ak->rkb", shaped, sin_one, precision=highest)
    cos_twist, sin_twist = phase_table(first, second, nfft)
    twist_real = section_real * cos_twist[None] + section_imag * sin_twist[None]
    twist_imag = section_imag * cos_twist[None] - section_real * sin_twist[None]
    cos_two, sin_two = phase_table(second, second // 2, second)
    out_real = jnp.einsum("rkb,bm->rmk", twist_real, cos_two, precision=highest) + jnp.einsum(
        "rkb,bm->rmk", twist_imag, sin_two, precision=highest
    )
    out_imag = jnp.einsum("rkb,bm->rmk", twist_imag, cos_two, precision=highest) - jnp.einsum(
        "rkb,bm->rmk", twist_real, sin_two, precision=highest
    )
    scale = 1.0 / math.sqrt(nfft)
    return (
        out_real.reshape(rows_count, nfft // 2) * scale,
        out_imag.reshape(rows_count, nfft // 2) * scale,
    )


def complex_product(weights, real_part, imag_part, form):
    w_real = weights[0]
    w_imag = weights[1]
    out_real = jnp.einsum(form, w_real, real_part, preferred_element_type=jnp.float32) - jnp.einsum(
        form, w_imag, imag_part, preferred_element_type=jnp.float32
    )
    out_imag = jnp.einsum(form, w_real, imag_part, preferred_element_type=jnp.float32) + jnp.einsum(
        form, w_imag, real_part, preferred_element_type=jnp.float32
    )
    return (out_real, out_imag)


def dedisperse(extended, delay_block, spec_dev, trials, scale):
    beam_count = extended.shape[2]

    def turn(shift_value, total):
        piece = lax.dynamic_slice_in_dim(extended, shift_value, spec_dev, 0)
        selector = (delay_block == shift_value).astype(jnp.bfloat16)
        return total + jnp.einsum(
            "scb,tc->bst", piece, selector, preferred_element_type=jnp.float32
        )

    summed = lax.fori_loop(
        0, spec_dev + 1, turn, jnp.zeros((beam_count, spec_dev, trials), jnp.float32)
    )
    return summed * scale


def plain_device(samples, fir_taps, beam_y, beam_x, delays):
    dish_dev, total_points = samples.shape
    taps_count, nfft = fir_taps.shape
    spec_dev = total_points // nfft
    side_x = beam_x.shape[1]
    side_y = beam_y.shape[1]
    trials, channels = delays.shape
    frames = samples.reshape(dish_dev, spec_dev, nfft)
    history = shifted(frames[:, spec_dev - taps_count + 1 :, :], "tm", 1)
    extended_frames = jnp.concatenate([history, frames], axis=1)
    filtered = jnp.zeros((dish_dev, spec_dev, nfft), jnp.float32)
    for tap_index in range(taps_count):
        offset = taps_count - 1 - tap_index
        filtered = filtered + fir_taps[tap_index][None, None, :] * extended_frames[
            :, offset : offset + spec_dev, :
        ].astype(jnp.float32)
    frame_rows = filtered.reshape(dish_dev * spec_dev, nfft)
    volt_real, volt_imag = transform(frame_rows, nfft)
    volts = jnp.stack(
        [
            volt_real.reshape(dish_dev, spec_dev, nfft // 2),
            volt_imag.reshape(dish_dev, spec_dev, nfft // 2),
        ],
        axis=2,
    ).astype(jnp.bfloat16)
    gathered = lax.all_to_all(volts, "chan", split_axis=3, concat_axis=0, tiled=True)
    items = gathered.shape[1]
    chan_dev = gathered.shape[3]
    grid = gathered.reshape(side_x, side_y, items, 2, chan_dev)
    part_real, part_imag = complex_product(
        beam_y, grid[:, :, :, 0], grid[:, :, :, 1], "py,xync->ncxp"
    )
    part_real = part_real.astype(jnp.bfloat16)
    part_imag = part_imag.astype(jnp.bfloat16)
    form_real, form_imag = complex_product(beam_x, part_real, part_imag, "qx,ncxp->ncqp")
    power = (form_real * form_real + form_imag * form_imag).reshape(
        items, chan_dev, side_x * side_y
    )
    powers = (power - jnp.mean(power, axis=2, keepdims=True)).astype(jnp.bfloat16)
    scale = 1.0 / math.sqrt(channels)
    chan_dev = powers.shape[1]
    following = shifted(powers, "tm", -1)
    extended = jnp.concatenate([powers, following], axis=0)
    local_delays = lax.dynamic_slice_in_dim(delays, lax.axis_index("chan") * chan_dev, chan_dev, 1)
    return lax.psum_scatter(
        dedisperse(extended, local_delays, spec_dev, trials, scale),
        "chan",
        scatter_dimension=0,
        tiled=True,
    )


def real_dft(parts):
    count = len(parts)
    if count == 1:
        return [(parts[0], None)]
    half = count // 2
    even = real_dft(parts[0::2])
    odd = real_dft(parts[1::2])
    out = [None] * (half + 1)
    for k in range(half // 2 + 1):
        even_re, even_im = even[k]
        odd_re, odd_im = odd[k]
        if k == 0:
            out[0] = (even_re + odd_re, None)
            out[half] = (even_re - odd_re, None)
        elif 4 * k == count:
            out[k] = (even_re, -odd_re)
        else:
            cos = math.cos(2.0 * math.pi * k / count)
            sin = math.sin(2.0 * math.pi * k / count)
            if 8 * k == count:
                turn_re = (odd_re + odd_im) * cos
                turn_im = (odd_im - odd_re) * cos
            else:
                turn_re = odd_re * cos + odd_im * sin
                turn_im = odd_im * cos - odd_re * sin
            out[k] = (even_re + turn_re, even_im + turn_im)
            out[half - k] = (even_re - turn_re, turn_im - even_im)
    return out


def dft_tables(nfft):
    radix = nfft // LANES
    point = np.arange(LANES)[:, None]
    column = np.arange(LANES)[None, :]
    scale = 1.0 / math.sqrt(nfft)
    angle = 2.0 * np.pi * ((point * column) % LANES) / LANES
    sign = np.where(column < LANES // 2, 1.0, -1.0)
    cos, sin = np.cos(angle), np.sin(angle)
    full = np.block([[cos, -sin * sign], [sin, cos * sign]]) * scale
    low = column < LANES // 2
    low_angle = 2.0 * np.pi * ((point * radix * column) % nfft) / nfft
    high_index = radix // 2 + radix * (column - LANES // 2)
    high_angle = 2.0 * np.pi * ((point * high_index) % nfft) / nfft
    edge = (
        np.block(
            [
                [np.where(low, np.cos(low_angle), 0.0), np.where(low, -np.sin(low_angle), 0.0)],
                [np.where(low, 0.0, np.cos(high_angle)), np.where(low, 0.0, -np.sin(high_angle))],
            ]
        )
        * scale
    )
    tables = np.stack([edge, full]).astype(np.float32)
    turn = 2.0 * np.pi * np.arange(radix // 2)[:, None] * np.arange(LANES)[None, :] / nfft
    twist = np.stack([np.cos(turn), np.sin(turn)]).astype(np.float32)
    return tables, twist


def split(value):
    high = value.astype(BF16)
    return high, (value - high.astype(F32)).astype(BF16)


def front_kernel(low_spec, taps_count, hist_list, hist_base, peers, pieces, *refs):
    own = refs[0]
    hists = refs[1 : 1 + hist_list]
    taps, twist, mat_high, mat_low, steer = refs[1 + hist_list : 6 + hist_list]
    outs = refs[6 + hist_list : 6 + hist_list + peers]
    ships = refs[6 + hist_list + peers : 6 + hist_list + peers + len(pieces)]
    win, filt, z_high, z_low, volt, sem, ship_sem = refs[6 + hist_list + peers + len(pieces) :]
    groups, frames, rows, nfft = win.shape
    slabs = z_high.shape[0]
    radix = nfft // LANES
    step = 16

    def fetch(group, index):
        frame = low_spec - taps_count + 1 + index
        row_block = pl.ds(group * rows, rows)
        if frame >= 0:
            source = own.at[row_block, pl.ds(frame * nfft, nfft)]
        else:
            which, place = hist_base[frame]
            source = hists[which].at[row_block, pl.ds(place * nfft, nfft)]
        return pltpu.make_async_copy(source, win.at[group, index], sem.at[group, index])

    for group in range(groups):
        for index in range(frames):
            fetch(group, index).start()

    def ship(group, which, place):
        index = pieces[which][0] + place
        return pltpu.make_async_copy(
            win.at[group, index],
            ships[which].at[pl.ds(group * rows, rows), pl.ds(place * nfft, nfft)],
            ship_sem.at[group, index],
        )

    every = [(which, place) for which, piece in enumerate(pieces) for place in range(piece[1])]

    def on_group(group, carry):
        for index in range(frames):
            fetch(group, index).wait()
        for which, place in every:
            ship(group, which, place).start()

        def on_spec(place, carry):
            def fir(block, carry):
                block_rows = pl.ds(pl.multiple_of(block * step, step), step)
                for tile in range(radix):
                    lanes = slice(tile * LANES, (tile + 1) * LANES)
                    total = None
                    for tap in range(taps_count):
                        piece = win[group, place + taps_count - 1 - tap, block_rows, lanes]
                        term = piece.astype(F32) * taps[tap : tap + 1, lanes]
                        total = term if total is None else total + term
                    filt[block_rows, lanes] = total
                return carry

            lax.fori_loop(0, rows // step, fir, 0)

            def turn(block, carry):
                block_rows = pl.ds(pl.multiple_of(block * step, step), step)
                bins = real_dft(
                    [filt[block_rows, tile * LANES : (tile + 1) * LANES] for tile in range(radix)]
                )
                for slab in range(slabs):
                    if slab == 0:
                        z_re, z_im = bins[0][0], bins[radix // 2][0]
                    else:
                        x_re, x_im = bins[slab]
                        cos = twist[0, slab : slab + 1, :]
                        sin = twist[1, slab : slab + 1, :]
                        z_re = x_re * cos + x_im * sin
                        z_im = x_im * cos - x_re * sin
                    high, low = split(z_re)
                    z_high[slab, block_rows, 0:LANES] = high
                    z_low[slab, block_rows, 0:LANES] = low
                    high, low = split(z_im)
                    z_high[slab, block_rows, LANES : 2 * LANES] = high
                    z_low[slab, block_rows, LANES : 2 * LANES] = low
                return carry

            lax.fori_loop(0, rows // step, turn, 0)

            def product(first, count, which):
                size = count * rows
                high = z_high[first : first + count].reshape(size, 2 * LANES)
                low = z_low[first : first + count].reshape(size, 2 * LANES)
                value = jnp.dot(high, mat_high[which], preferred_element_type=F32)
                value += jnp.dot(low, mat_high[which], preferred_element_type=F32)
                value += jnp.dot(high, mat_low[which], preferred_element_type=F32)
                volt[first : first + count] = value.astype(BF16).reshape(count, rows, 2 * LANES)

            product(0, 1, 0)
            batch = 3 if (slabs - 1) % 3 == 0 else 1
            for first in range(1, slabs, batch):
                product(first, batch, 1)

            for slab in range(0, slabs, 2):
                data = jnp.concatenate(
                    [
                        jnp.concatenate([volt[at, :, 0:LANES], volt[at, :, LANES:]], axis=0)
                        for at in (slab, slab + 1)
                    ],
                    axis=1,
                )
                beams = jnp.dot(steer[...], data, preferred_element_type=F32).astype(BF16)
                tile_rows = 2 * PAIR * GROUP_X
                pairs = steer.shape[0] // (peers * tile_rows)
                beams = beams.reshape(peers, pairs, tile_rows, 2 * LANES)
                for peer in range(peers):
                    for pair in range(pairs):
                        outs[peer][
                            place, pair, group, :, slab * LANES : (slab + 2) * LANES
                        ] = beams[peer, pair]
            return carry

        lax.fori_loop(0, frames - taps_count + 1, on_spec, 0)
        return carry

    lax.fori_loop(0, groups, on_group, 0)
    for group in range(groups):
        for which, place in every:
            ship(group, which, place).wait()


def front(own, hists, hist_base, taps, twist, mat_high, mat_low, steer, low_spec, specs, peers, pairs, pieces):
    taps_count, nfft = taps.shape
    dishes = own.shape[0]
    rows = steer.shape[1] // 2
    groups = dishes // rows
    frames = taps_count + specs - 1
    slabs = nfft // LANES // 2
    channels = nfft // 2
    any_space = pl.BlockSpec(memory_space=pl.ANY)
    vmem = pl.BlockSpec(memory_space=pltpu.VMEM)
    flops = 2 * specs * dishes * slabs * 3 * (2 * LANES) ** 2 + 2 * specs * groups * slabs * LANES * steer.size
    return pl.pallas_call(
        functools.partial(front_kernel, low_spec, taps_count, len(hists), hist_base, peers, pieces),
        out_shape=[
            jax.ShapeDtypeStruct((specs, pairs, groups, 2 * PAIR * GROUP_X, channels), BF16)
            for _ in range(peers)
        ]
        + [jax.ShapeDtypeStruct((dishes, count * nfft), BF16) for _, count in pieces],
        in_specs=[any_space] * (1 + len(hists)) + [vmem] * 5,
        out_specs=[vmem] * peers + [any_space] * len(pieces),
        scratch_shapes=[
            pltpu.VMEM((groups, frames, rows, nfft), BF16),
            pltpu.VMEM((rows, nfft), F32),
            pltpu.VMEM((slabs, rows, 2 * LANES), BF16),
            pltpu.VMEM((slabs, rows, 2 * LANES), BF16),
            pltpu.VMEM((slabs, rows, 2 * LANES), BF16),
            pltpu.SemaphoreType.DMA((groups, frames)),
            pltpu.SemaphoreType.DMA((groups, frames)),
        ],
        compiler_params=pltpu.CompilerParams(vmem_limit_bytes=56 * 1024 * 1024),
        cost_estimate=pl.CostEstimate(
            flops=flops, bytes_accessed=dishes * nfft * 2 * (frames + specs), transcendentals=0
        ),
    )(own, *hists, taps, twist, mat_high, mat_low, steer)


def back_kernel(low_spec, specs, span, peers, first, last, *refs):
    parts = refs[:peers]
    if last:
        refs, (early, own) = refs[:-6] + (refs[-1],) + refs[-4:-1], refs[-6:-4]
    if first:
        steer, delays, total, p_high, p_low, chosen = refs[peers:]
        total[...] = jnp.zeros_like(total)
    else:
        steer, delays, before, total, p_high, p_low, chosen = refs[peers:]
        total[...] = before[...]
    _, pairs, groups, _, channels = parts[0].shape
    out_rows = steer.shape[0] // 2
    width = chosen.shape[1]
    trials = LANES // 2
    step = 512
    upper = lax.broadcasted_iota(jnp.int32, (1, LANES), 1) >= trials
    for place in range(specs):
        spec = low_spec + place
        for pair in range(pairs):
            for start in range(0, channels, step):
                lanes = slice(start, start + step)
                data = jnp.concatenate(
                    [
                        parts[peer][place, pair, group, :, lanes]
                        for peer in range(peers)
                        for group in range(groups)
                    ],
                    axis=0,
                )
                formed = jnp.dot(steer[...], data, preferred_element_type=F32)
                power = formed[:out_rows] * formed[:out_rows] + formed[out_rows:] * formed[out_rows:]
                high, low = split(power)
                pair_rows = slice(pair * out_rows, (pair + 1) * out_rows)
                p_high[pair_rows, lanes] = high
                p_low[pair_rows, lanes] = low
        odd = spec % 2
        for tile in range(width // LANES):
            top = span + odd - 2 * tile
            wanted = jnp.where(upper, top - 1, top)
            chosen[:, tile * LANES : (tile + 1) * LANES] = jnp.where(
                delays[...] == wanted, 1.0, 0.0
            ).astype(BF16)
        base = (spec - odd) * trials
        start = 0
        while start < width:
            size = min(2 * LANES, width - start)
            weights = chosen[:, start : start + size]
            value = jnp.dot(p_high[...], weights, preferred_element_type=F32)
            value += jnp.dot(p_low[...], weights, preferred_element_type=F32)
            total[:, base + start : base + start + size] += value
            start += size
    if last:
        half = total.shape[1] // 2
        early[...] = total[:, :half]
        own[...] = total[:, half:]


def back(parts, steer, delays, before, low_spec, span, last):
    peers = len(parts)
    specs, pairs, _, _, channels = parts[0].shape
    beams = pairs * steer.shape[0] // 2
    width = (span + 2) * LANES // 2
    shape = (beams, 2 * span * LANES // 2)
    vmem = pl.BlockSpec(memory_space=pltpu.VMEM)
    first = before is None
    extra = () if first else (before,)
    flops = 2 * specs * (pairs * steer.size * channels + 2 * beams * channels * width)
    return pl.pallas_call(
        functools.partial(back_kernel, low_spec, specs, span, peers, first, last),
        out_shape=[jax.ShapeDtypeStruct((beams, shape[1] // 2), F32)] * 2
        if last
        else jax.ShapeDtypeStruct(shape, F32),
        in_specs=[vmem] * (peers + 2 + len(extra)),
        out_specs=[vmem, vmem] if last else vmem,
        scratch_shapes=[
            pltpu.VMEM((beams, channels), BF16),
            pltpu.VMEM((beams, channels), BF16),
            pltpu.VMEM((channels, width), BF16),
        ]
        + ([pltpu.VMEM(shape, F32)] if last else []),
        compiler_params=pltpu.CompilerParams(vmem_limit_bytes=48 * 1024 * 1024),
        cost_estimate=pl.CostEstimate(
            flops=flops, bytes_accessed=peers * parts[0].size * 2, transcendentals=0
        ),
    )(*parts, steer, delays, *extra)


def deal_kernel(peers, me, own, came, *refs):
    outs = refs[:peers]
    total = refs[peers]
    beams, width = own.shape
    side_x = 8 * peers
    side_p = beams // side_x
    total[...] = own[...] + came[...]
    summed = jnp.broadcast_to(jnp.sum(total[...], axis=0, keepdims=True), (8, width))
    for peer in range(peers):
        target = lax.rem(me[0] + peer, peers)
        for at in range(side_p):
            outs[peer][8 * at : 8 * at + 8, :] = total[
                pl.ds(pl.multiple_of(at * side_x + target * 8, 8), 8), :
            ]
        outs[peer][8 * side_p : 8 * side_p + 8, :] = summed


def join_kernel(peers, scale, beams_all, me, *refs):
    parts = refs[:peers]
    out = refs[peers]
    side_p = parts[0].shape[0] // 8 - 1
    mean = parts[0][8 * side_p : 8 * side_p + 8, :]
    for peer in range(1, peers):
        mean = mean + parts[peer][8 * side_p : 8 * side_p + 8, :]
    mean = mean * (1.0 / beams_all)
    for peer in range(peers):
        source = lax.rem(me[0] + peers - peer, peers)
        for at in range(side_p):
            value = (parts[peer][8 * at : 8 * at + 8, :] - mean) * scale
            for row in range(8):
                out[pl.ds(row * side_p * peers + source * side_p + at, 1), :] = value[row : row + 1, :]


def fast_device(samples, fir_taps, beam_y, beam_x, delays):
    dishes, points = samples.shape
    taps_count, nfft = fir_taps.shape
    span = points // nfft
    side_x, side_y = beam_x.shape[1], beam_y.shape[1]
    trials, channels = delays.shape
    peers = lax.axis_size("chan")
    me = lax.axis_index("chan")
    side_p = side_y // peers
    pairs = side_p // PAIR
    groups = dishes // side_y // GROUP_X
    radix = nfft // LANES

    chunks = []
    top, size = span, 1
    while top > 0:
        size = 1 if top == 1 else min(size, top - 1)
        chunks.append((top - size, size))
        top, size = top - size, 2 * size

    tables, twist = dft_tables(nfft)
    mat_high = tables.astype(BF16)
    mat_low = (tables - mat_high.astype(np.float32)).astype(BF16)

    real, imag = beam_y[0], beam_y[1]
    blocks = jnp.stack([jnp.stack([real, -imag]), jnp.stack([imag, real])])
    blocks = jnp.concatenate([blocks, blocks], axis=2)
    blocks = lax.dynamic_slice_in_dim(blocks, me * side_p, side_y, 2)
    blocks = blocks.transpose(2, 0, 1, 3)[:, :, None, :, None, :]
    eye = jnp.asarray(np.eye(GROUP_X), BF16)[None, None, :, None, :, None]
    steer_y = (blocks * eye).reshape(side_y * 2 * GROUP_X, 2 * GROUP_X * side_y)

    count_tm = lax.axis_size("tm")
    forward = [(i, i + 1) for i in range(count_tm - 1)]
    bounds = sorted({low - taps_count + 1 for low, _ in chunks[1:]}, reverse=True)
    bounds = [bound for bound in bounds if bound < 0]
    bounds = bounds[:2] + bounds[-1:] if len(bounds) > 3 else bounds
    hists, hist_base, pieces = [], {}, []
    upper = 0
    for bound in bounds:
        for frame in range(bound, upper):
            hist_base[frame] = (len(pieces), frame - bound)
        first_low = chunks[0][0] - taps_count + 1
        pieces.append((span + bound - first_low, upper - bound))
        upper = bound
    total = None
    sent = []
    for at, (low_spec, specs) in enumerate(chunks):
        frames = range(low_spec - taps_count + 1, low_spec + specs)
        used = sorted({hist_base[f][0] for f in frames if f < 0})
        base = {f: (used.index(hist_base[f][0]), hist_base[f][1]) for f in frames if f < 0}
        outs = front(
            samples, [hists[i] for i in used], base, fir_taps, twist, mat_high, mat_low, steer_y,
            low_spec, specs, peers, pairs, () if at else tuple(pieces),
        )
        order = sorted(range(1, peers), key=lambda r: abs(r - peers // 2))
        got = [outs[0]] + [None] * (peers - 1)
        for shift in order:
            got[shift] = lax.ppermute(
                outs[shift], "chan", [(i, (i + shift) % peers) for i in range(peers)]
            )
        sent.append((low_spec, got))
        if at == 0:
            for which in range(len(pieces)):
                hists.append(lax.ppermute(outs[peers + which], "tm", forward))
    delays, beam_x, sent[-1][1][0] = lax.optimization_barrier((delays, beam_x, sent[-1][1][0]))
    real, imag = beam_x[0], beam_x[1]
    blocks = jnp.stack([jnp.stack([real, -imag]), jnp.stack([imag, real])])
    blocks = blocks.reshape(2, 2, side_x, peers, groups, GROUP_X)[:, :, :, ::-1]
    blocks = jnp.concatenate([blocks, blocks], axis=3)
    blocks = lax.dynamic_slice_in_dim(blocks, peers - 1 - me, peers, 3)
    blocks = blocks.transpose(0, 2, 3, 4, 1, 5)[:, None, :, :, :, None, :, :]
    eye = jnp.asarray(np.eye(PAIR), BF16)[None, :, None, None, None, :, None, None]
    steer_x = (blocks * eye).reshape(2 * PAIR * side_x, peers * groups * PAIR * 2 * GROUP_X)

    by_bin = delays.reshape(trials, channels // radix, radix).transpose(2, 1, 0)
    folded = jnp.concatenate([by_bin[radix // 2 : radix // 2 + 1], by_bin[radix // 2 + 1 :][::-1, ::-1]])
    ordered = jnp.concatenate([by_bin[: radix // 2], folded], axis=1).reshape(channels, trials)
    ordered = jnp.concatenate([ordered, ordered], axis=1)

    for low_spec, got in sent:
        total = back(got, steer_x, ordered, total, low_spec, span, low_spec == 0)
    early, own = total

    width = span * trials
    came = lax.ppermute(early, "tm", [(i + 1, i) for i in range(count_tm - 1)])
    spot = me.reshape(1)
    smem = pl.BlockSpec(memory_space=pltpu.SMEM)
    vmem = pl.BlockSpec(memory_space=pltpu.VMEM)
    rows = 8 * (side_p + 1)
    dealt = pl.pallas_call(
        functools.partial(deal_kernel, peers),
        out_shape=[jax.ShapeDtypeStruct((rows, width), F32) for _ in range(peers)],
        in_specs=[smem, vmem, vmem],
        out_specs=[vmem] * peers,
        scratch_shapes=[pltpu.VMEM(own.shape, F32)],
        name="deal",
    )(spot, own, came)
    joined = [dealt[0]]
    joined += [None] * (peers - 1)
    for shift in order:
        joined[shift] = lax.ppermute(
            dealt[shift], "chan", [(i, (i + shift) % peers) for i in range(peers)]
        )
    series = pl.pallas_call(
        functools.partial(join_kernel, peers, 1.0 / math.sqrt(channels), side_x * side_y),
        out_shape=jax.ShapeDtypeStruct((own.shape[0], width), F32),
        in_specs=[smem] + [vmem] * peers,
        out_specs=vmem,
        name="join",
    )(spot, *joined)
    return series.reshape(own.shape[0], span, trials)


def on_device(samples, fir_taps, beam_y, beam_x, delays):
    dishes, points = samples.shape
    taps_count, nfft = fir_taps.shape
    side_x, side_y = beam_x.shape[1], beam_y.shape[1]
    trials, channels = delays.shape
    peers = lax.axis_size("chan")
    span = points // nfft
    fits = (
        dishes % (side_y * GROUP_X) == 0
        and side_y % (peers * PAIR) == 0
        and side_x == 8 * peers
        and 2 * trials == LANES
        and nfft % (4 * LANES) == 0
        and channels * 2 == nfft
        and span % 2 == 0
        and taps_count - 1 <= span
    )
    if fits:
        return fast_device(samples, fir_taps, beam_y, beam_x, delays)
    return plain_device(samples, fir_taps, beam_y, beam_x, delays)


def solution(mesh):
    return jax.shard_map(
        on_device,
        mesh=mesh,
        in_specs=(P("chan", "tm"), P(), P(), P(), P()),
        out_specs=P("chan", "tm", None),
        check_vma=False,
    )
```

```python
import functools
import math

import jax
import jax.numpy as jnp
import numpy as np
from jax import lax
from jax.experimental import pallas as pl
from jax.experimental.pallas import tpu as pltpu
from jax.sharding import PartitionSpec as P


LANES = 128
GROUP_X = 4
PAIR = 2
PARTS = 8
BF16 = jnp.bfloat16
F32 = jnp.float32


def shifted(array, axis, by):
    count = lax.axis_size(axis)
    pairs = [(i, i + by) for i in range(count) if 0 <= i + by < count]
    return lax.ppermute(array, axis, pairs)


def phase_table(rows_count, cols_count, period):
    row_index = jnp.arange(rows_count, dtype=jnp.int32)[:, None]
    col_index = jnp.arange(cols_count, dtype=jnp.int32)[None, :]
    angle = (row_index * col_index % period).astype(jnp.float32) * (2.0 * math.pi / period)
    return (jnp.cos(angle), jnp.sin(angle))


def transform(frames_rows, nfft):
    bits = nfft.bit_length() - 1
    first = 1 << bits // 2
    second = nfft // first
    rows_count = frames_rows.shape[0]
    shaped = frames_rows.reshape(rows_count, first, second)
    highest = lax.Precision.HIGHEST
    cos_one, sin_one = phase_table(first, first, first)
    section_real = jnp.einsum("rab,ak->rkb", shaped, cos_one, precision=highest)
    section_imag = -jnp.einsum("rab,ak->rkb", shaped, sin_one, precision=highest)
    cos_twist, sin_twist = phase_table(first, second, nfft)
    twist_real = section_real * cos_twist[None] + section_imag * sin_twist[None]
    twist_imag = section_imag * cos_twist[None] - section_real * sin_twist[None]
    cos_two, sin_two = phase_table(second, second // 2, second)
    out_real = jnp.einsum("rkb,bm->rmk", twist_real, cos_two, precision=highest) + jnp.einsum(
        "rkb,bm->rmk", twist_imag, sin_two, precision=highest
    )
    out_imag = jnp.einsum("rkb,bm->rmk", twist_imag, cos_two, precision=highest) - jnp.einsum(
        "rkb,bm->rmk", twist_real, sin_two, precision=highest
    )
    scale = 1.0 / math.sqrt(nfft)
    return (
        out_real.reshape(rows_count, nfft // 2) * scale,
        out_imag.reshape(rows_count, nfft // 2) * scale,
    )


def complex_product(weights, real_part, imag_part, form):
    w_real = weights[0]
    w_imag = weights[1]
    out_real = jnp.einsum(form, w_real, real_part, preferred_element_type=jnp.float32) - jnp.einsum(
        form, w_imag, imag_part, preferred_element_type=jnp.float32
    )
    out_imag = jnp.einsum(form, w_real, imag_part, preferred_element_type=jnp.float32) + jnp.einsum(
        form, w_imag, real_part, preferred_element_type=jnp.float32
    )
    return (out_real, out_imag)


def dedisperse(extended, delay_block, spec_dev, trials, scale):
    beam_count = extended.shape[2]

    def turn(shift_value, total):
        piece = lax.dynamic_slice_in_dim(extended, shift_value, spec_dev, 0)
        selector = (delay_block == shift_value).astype(jnp.bfloat16)
        return total + jnp.einsum(
            "scb,tc->bst", piece, selector, preferred_element_type=jnp.float32
        )

    summed = lax.fori_loop(
        0, spec_dev + 1, turn, jnp.zeros((beam_count, spec_dev, trials), jnp.float32)
    )
    return summed * scale


def plain_device(samples, fir_taps, beam_y, beam_x, delays):
    dish_dev, total_points = samples.shape
    taps_count, nfft = fir_taps.shape
    spec_dev = total_points // nfft
    side_x = beam_x.shape[1]
    side_y = beam_y.shape[1]
    trials, channels = delays.shape
    frames = samples.reshape(dish_dev, spec_dev, nfft)
    history = shifted(frames[:, spec_dev - taps_count + 1 :, :], "tm", 1)
    extended_frames = jnp.concatenate([history, frames], axis=1)
    filtered = jnp.zeros((dish_dev, spec_dev, nfft), jnp.float32)
    for tap_index in range(taps_count):
        offset = taps_count - 1 - tap_index
        filtered = filtered + fir_taps[tap_index][None, None, :] * extended_frames[
            :, offset : offset + spec_dev, :
        ].astype(jnp.float32)
    frame_rows = filtered.reshape(dish_dev * spec_dev, nfft)
    volt_real, volt_imag = transform(frame_rows, nfft)
    volts = jnp.stack(
        [
            volt_real.reshape(dish_dev, spec_dev, nfft // 2),
            volt_imag.reshape(dish_dev, spec_dev, nfft // 2),
        ],
        axis=2,
    ).astype(jnp.bfloat16)
    gathered = lax.all_to_all(volts, "chan", split_axis=3, concat_axis=0, tiled=True)
    items = gathered.shape[1]
    chan_dev = gathered.shape[3]
    grid = gathered.reshape(side_x, side_y, items, 2, chan_dev)
    part_real, part_imag = complex_product(
        beam_y, grid[:, :, :, 0], grid[:, :, :, 1], "py,xync->ncxp"
    )
    part_real = part_real.astype(jnp.bfloat16)
    part_imag = part_imag.astype(jnp.bfloat16)
    form_real, form_imag = complex_product(beam_x, part_real, part_imag, "qx,ncxp->ncqp")
    power = (form_real * form_real + form_imag * form_imag).reshape(
        items, chan_dev, side_x * side_y
    )
    powers = (power - jnp.mean(power, axis=2, keepdims=True)).astype(jnp.bfloat16)
    scale = 1.0 / math.sqrt(channels)
    chan_dev = powers.shape[1]
    following = shifted(powers, "tm", -1)
    extended = jnp.concatenate([powers, following], axis=0)
    local_delays = lax.dynamic_slice_in_dim(delays, lax.axis_index("chan") * chan_dev, chan_dev, 1)
    return lax.psum_scatter(
        dedisperse(extended, local_delays, spec_dev, trials, scale),
        "chan",
        scatter_dimension=0,
        tiled=True,
    )


def real_dft(parts):
    count = len(parts)
    if count == 1:
        return [(parts[0], None)]
    half = count // 2
    even = real_dft(parts[0::2])
    odd = real_dft(parts[1::2])
    out = [None] * (half + 1)
    for k in range(half // 2 + 1):
        even_re, even_im = even[k]
        odd_re, odd_im = odd[k]
        if k == 0:
            out[0] = (even_re + odd_re, None)
            out[half] = (even_re - odd_re, None)
        elif 4 * k == count:
            out[k] = (even_re, -odd_re)
        else:
            cos = math.cos(2.0 * math.pi * k / count)
            sin = math.sin(2.0 * math.pi * k / count)
            if 8 * k == count:
                turn_re = (odd_re + odd_im) * cos
                turn_im = (odd_im - odd_re) * cos
            else:
                turn_re = odd_re * cos + odd_im * sin
                turn_im = odd_im * cos - odd_re * sin
            out[k] = (even_re + turn_re, even_im + turn_im)
            out[half - k] = (even_re - turn_re, turn_im - even_im)
    return out


def dft_tables(nfft):
    radix = nfft // LANES
    point = np.arange(LANES)[:, None]
    column = np.arange(LANES)[None, :]
    scale = 1.0 / math.sqrt(nfft)
    angle = 2.0 * np.pi * ((point * column) % LANES) / LANES
    sign = np.where(column < LANES // 2, 1.0, -1.0)
    cos, sin = np.cos(angle), np.sin(angle)
    full = np.block([[cos, -sin * sign], [sin, cos * sign]]) * scale
    low = column < LANES // 2
    low_angle = 2.0 * np.pi * ((point * radix * column) % nfft) / nfft
    high_index = radix // 2 + radix * (column - LANES // 2)
    high_angle = 2.0 * np.pi * ((point * high_index) % nfft) / nfft
    edge = (
        np.block(
            [
                [np.where(low, np.cos(low_angle), 0.0), np.where(low, -np.sin(low_angle), 0.0)],
                [np.where(low, 0.0, np.cos(high_angle)), np.where(low, 0.0, -np.sin(high_angle))],
            ]
        )
        * scale
    )
    tables = np.stack([edge, full]).astype(np.float32)
    turn = 2.0 * np.pi * np.arange(radix // 2)[:, None] * np.arange(LANES)[None, :] / nfft
    twist = np.stack([np.cos(turn), np.sin(turn)]).astype(np.float32)
    return tables, twist


def split(value):
    high = value.astype(BF16)
    return high, (value - high.astype(F32)).astype(BF16)


def build_steer(peers, me, beam, steer):
    side = beam.shape[1]
    shape = steer.shape
    unit = 2 * GROUP_X
    row = lax.broadcasted_iota(jnp.int32, (shape[0], side), 0)
    picked = lax.rem(me[0] * (side // peers) + row // unit, side)
    pick = (lax.broadcasted_iota(jnp.int32, (shape[0], side), 1) == picked).astype(F32).astype(BF16)
    column = lax.broadcasted_iota(jnp.int32, (side, shape[1]), 1)
    spread = lax.broadcasted_iota(jnp.int32, (side, shape[1]), 0) == lax.rem(column, side)
    spread = spread.astype(F32).astype(BF16)
    real, imag = [
        jnp.dot(
            jnp.dot(pick, beam[part], preferred_element_type=F32).astype(BF16),
            spread,
            preferred_element_type=F32,
        )
        for part in range(2)
    ]
    row = lax.broadcasted_iota(jnp.int32, shape, 0)
    column = lax.broadcasted_iota(jnp.int32, shape, 1)
    row_part = lax.rem(row // GROUP_X, 2)
    column_part = column // (GROUP_X * side)
    same_dish = lax.rem(row, GROUP_X) == lax.rem(column // side, GROUP_X)
    value = jnp.where(row_part == column_part, real, jnp.where(row_part == 0, -imag, imag))
    steer[...] = jnp.where(same_dish, value, 0.0).astype(BF16)


def front_kernel(low_spec, taps_count, hist_list, hist_base, peers, pieces, *refs):
    me, own = refs[:2]
    refs = refs[1:]
    hists = refs[1 : 1 + hist_list]
    taps, twist, mat_high, mat_low, beam = refs[1 + hist_list : 6 + hist_list]
    outs = refs[6 + hist_list : 6 + hist_list + peers]
    ships = refs[6 + hist_list + peers : 6 + hist_list + peers + len(pieces)]
    win, filt, z_high, z_low, volt, steer, sem, ship_sem = refs[6 + hist_list + peers + len(pieces) :]
    groups, frames, rows, nfft = win.shape
    slabs = z_high.shape[0]
    radix = nfft // LANES
    step = 16
    part_rows = rows // PARTS

    def fetch(group, part, index):
        frame = low_spec - taps_count + 1 + index
        row_block = pl.ds(group * rows + part * part_rows, part_rows)
        if frame >= 0:
            source = own.at[row_block, pl.ds(frame * nfft, nfft)]
        else:
            which, place = hist_base[frame]
            source = hists[which].at[row_block, pl.ds(place * nfft, nfft)]
        target = win.at[group, index, pl.ds(part * part_rows, part_rows)]
        return pltpu.make_async_copy(source, target, sem.at[group, part, index])

    for group in range(groups):
        for part in range(PARTS):
            for index in range(frames):
                fetch(group, part, index).start()
    build_steer(peers, me, beam, steer)

    def ship(group, which, place):
        index = pieces[which][0] + place
        return pltpu.make_async_copy(
            win.at[group, index],
            ships[which].at[pl.ds(group * rows, rows), pl.ds(place * nfft, nfft)],
            ship_sem.at[group, index],
        )

    every = [(which, place) for which, piece in enumerate(pieces) for place in range(piece[1])]

    def on_group(group, carry):
        def on_spec(place, carry):
            def fir(block, carry):
                blocks = part_rows // step

                @pl.when((place == 0) & (lax.rem(block, blocks) == 0))
                def _():
                    for index in range(frames):
                        fetch(group, block // blocks, index).wait()

                block_rows = pl.ds(pl.multiple_of(block * step, step), step)
                for tile in range(radix):
                    lanes = slice(tile * LANES, (tile + 1) * LANES)
                    total = None
                    for tap in range(taps_count):
                        piece = win[group, place + taps_count - 1 - tap, block_rows, lanes]
                        term = piece.astype(F32) * taps[tap : tap + 1, lanes]
                        total = term if total is None else total + term
                    filt[block_rows, lanes] = total
                return carry

            lax.fori_loop(0, rows // step, fir, 0)
            if every:

                @pl.when(place == 0)
                def _():
                    for which, at in every:
                        ship(group, which, at).start()

            def turn(block, carry):
                block_rows = pl.ds(pl.multiple_of(block * step, step), step)
                bins = real_dft(
                    [filt[block_rows, tile * LANES : (tile + 1) * LANES] for tile in range(radix)]
                )
                for slab in range(slabs):
                    if slab == 0:
                        z_re, z_im = bins[0][0], bins[radix // 2][0]
                    else:
                        x_re, x_im = bins[slab]
                        cos = twist[0, slab : slab + 1, :]
                        sin = twist[1, slab : slab + 1, :]
                        z_re = x_re * cos + x_im * sin
                        z_im = x_im * cos - x_re * sin
                    high, low = split(z_re)
                    z_high[slab, block_rows, 0:LANES] = high
                    z_low[slab, block_rows, 0:LANES] = low
                    high, low = split(z_im)
                    z_high[slab, block_rows, LANES : 2 * LANES] = high
                    z_low[slab, block_rows, LANES : 2 * LANES] = low
                return carry

            lax.fori_loop(0, rows // step, turn, 0)

            def product(first, count, which):
                size = count * rows
                high = z_high[first : first + count].reshape(size, 2 * LANES)
                low = z_low[first : first + count].reshape(size, 2 * LANES)
                value = jnp.dot(high, mat_high[which], preferred_element_type=F32)
                value += jnp.dot(low, mat_high[which], preferred_element_type=F32)
                value += jnp.dot(high, mat_low[which], preferred_element_type=F32)
                volt[first : first + count] = value.astype(BF16).reshape(count, rows, 2 * LANES)

            product(0, 1, 0)
            batch = 3 if (slabs - 1) % 3 == 0 else 1
            for first in range(1, slabs, batch):
                product(first, batch, 1)

            for slab in range(0, slabs, 2):
                data = jnp.concatenate(
                    [
                        jnp.concatenate([volt[at, :, 0:LANES], volt[at, :, LANES:]], axis=0)
                        for at in (slab, slab + 1)
                    ],
                    axis=1,
                )
                beams = jnp.dot(steer[...], data, preferred_element_type=F32).astype(BF16)
                tile_rows = 2 * PAIR * GROUP_X
                pairs = steer.shape[0] // (peers * tile_rows)
                beams = beams.reshape(peers, pairs, tile_rows, 2 * LANES)
                for peer in range(peers):
                    for pair in range(pairs):
                        outs[peer][
                            place, pair, group, :, slab * LANES : (slab + 2) * LANES
                        ] = beams[peer, pair]
            return carry

        lax.fori_loop(0, frames - taps_count + 1, on_spec, 0)
        return carry

    lax.fori_loop(0, groups, on_group, 0)
    for group in range(groups):
        for which, place in every:
            ship(group, which, place).wait()


def front(own, hists, hist_base, taps, twist, mat_high, mat_low, beam, spot, low_spec, specs, peers, pairs, pieces):
    taps_count, nfft = taps.shape
    dishes = own.shape[0]
    side_y = beam.shape[1]
    rows = GROUP_X * side_y
    groups = dishes // rows
    frames = taps_count + specs - 1
    slabs = nfft // LANES // 2
    channels = nfft // 2
    any_space = pl.BlockSpec(memory_space=pl.ANY)
    vmem = pl.BlockSpec(memory_space=pltpu.VMEM)
    flops = 2 * specs * dishes * slabs * 3 * (2 * LANES) ** 2 + 2 * specs * groups * slabs * LANES * 4 * rows * rows
    return pl.pallas_call(
        functools.partial(front_kernel, low_spec, taps_count, len(hists), hist_base, peers, pieces),
        out_shape=[
            jax.ShapeDtypeStruct((specs, pairs, groups, 2 * PAIR * GROUP_X, channels), BF16)
            for _ in range(peers)
        ]
        + [jax.ShapeDtypeStruct((dishes, count * nfft), BF16) for _, count in pieces],
        in_specs=[pl.BlockSpec(memory_space=pltpu.SMEM)]
        + [any_space] * (1 + len(hists))
        + [vmem] * 5,
        out_specs=[vmem] * peers + [any_space] * len(pieces),
        scratch_shapes=[
            pltpu.VMEM((groups, frames, rows, nfft), BF16),
            pltpu.VMEM((rows, nfft), F32),
            pltpu.VMEM((slabs, rows, 2 * LANES), BF16),
            pltpu.VMEM((slabs, rows, 2 * LANES), BF16),
            pltpu.VMEM((slabs, rows, 2 * LANES), BF16),
            pltpu.VMEM((side_y * 2 * GROUP_X, 2 * GROUP_X * side_y), BF16),
            pltpu.SemaphoreType.DMA((groups, PARTS, frames)),
            pltpu.SemaphoreType.DMA((groups, frames)),
        ],
        compiler_params=pltpu.CompilerParams(vmem_limit_bytes=56 * 1024 * 1024),
        cost_estimate=pl.CostEstimate(
            flops=flops, bytes_accessed=dishes * nfft * 2 * (frames + specs), transcendentals=0
        ),
    )(spot, own, *hists, taps, twist, mat_high, mat_low, beam)


def back_kernel(low_spec, specs, span, peers, first, last, *refs):
    parts = refs[:peers]
    if last:
        refs, (early, own) = refs[:-5] + (refs[-1],) + refs[-3:-1], refs[-5:-3]
    if first:
        steer, delays, total, powers, chosen = refs[peers:]
        total[...] = jnp.zeros_like(total)
    else:
        steer, delays, before, total, powers, chosen = refs[peers:]
        total[...] = before[...]
    _, pairs, groups, _, channels = parts[0].shape
    out_rows = steer.shape[0] // 2
    beams = pairs * out_rows
    width = chosen.shape[1]
    trials = LANES // 2
    step = 512
    upper = lax.broadcasted_iota(jnp.int32, (1, LANES), 1) >= trials

    def on_spec(place, carry):
        spec = low_spec + place
        for pair in range(pairs):
            for start in range(0, channels, step):
                lanes = slice(start, start + step)
                data = jnp.concatenate(
                    [
                        parts[peer][place, pair, group, :, lanes]
                        for peer in range(peers)
                        for group in range(groups)
                    ],
                    axis=0,
                )
                formed = jnp.dot(steer[...], data, preferred_element_type=F32)
                power = formed[:out_rows] * formed[:out_rows] + formed[out_rows:] * formed[out_rows:]
                high, low = split(power)
                powers[pair * out_rows : (pair + 1) * out_rows, lanes] = high
                powers[beams + pair * out_rows : beams + (pair + 1) * out_rows, lanes] = low
        odd = lax.rem(spec, 2)
        for tile in range(width // LANES):
            top = span + odd - 2 * tile
            wanted = jnp.where(upper, top - 1, top)
            chosen[:, tile * LANES : (tile + 1) * LANES] = jnp.where(
                delays[...] == wanted, 1.0, 0.0
            ).astype(BF16)
        base = (spec - odd) * trials
        start = 0
        while start < width:
            size = min(2 * LANES, width - start)
            weights = chosen[:, start : start + size]
            value = jnp.dot(powers[...], weights, preferred_element_type=F32)
            lanes = pl.ds(pl.multiple_of(base + start, LANES), size)
            total[:, lanes] += value[:beams] + value[beams:]
            start += size
        return carry

    if specs == 1:
        on_spec(0, 0)
    else:
        lax.fori_loop(0, specs, on_spec, 0)
    if last:
        half = total.shape[1] // 2
        early[...] = total[:, :half]
        own[...] = total[:, half:]


def back(parts, steer, delays, before, low_spec, span, last):
    peers = len(parts)
    specs, pairs, _, _, channels = parts[0].shape
    beams = pairs * steer.shape[0] // 2
    width = (span + 2) * LANES // 2
    shape = (beams, 2 * span * LANES // 2)
    vmem = pl.BlockSpec(memory_space=pltpu.VMEM)
    first = before is None
    extra = () if first else (before,)
    flops = 2 * specs * (pairs * steer.size * channels + 2 * beams * channels * width)
    return pl.pallas_call(
        functools.partial(back_kernel, low_spec, specs, span, peers, first, last),
        out_shape=[jax.ShapeDtypeStruct((beams, shape[1] // 2), F32)] * 2
        if last
        else jax.ShapeDtypeStruct(shape, F32),
        in_specs=[vmem] * (peers + 2 + len(extra)),
        out_specs=[vmem, vmem] if last else vmem,
        scratch_shapes=[
            pltpu.VMEM((2 * beams, channels), BF16),
            pltpu.VMEM((channels, width), BF16),
        ]
        + ([pltpu.VMEM(shape, F32)] if last else []),
        compiler_params=pltpu.CompilerParams(vmem_limit_bytes=48 * 1024 * 1024),
        cost_estimate=pl.CostEstimate(
            flops=flops, bytes_accessed=peers * parts[0].size * 2, transcendentals=0
        ),
    )(*parts, steer, delays, *extra)


def deal_kernel(peers, me, own, came, *refs):
    outs = refs[:peers]
    total = refs[peers]
    beams, width = own.shape
    tiles = width // LANES
    side_x = 8 * peers
    side_p = beams // side_x
    total[...] = own[...] + came[...]
    summed = jnp.sum(total[...], axis=0, keepdims=True)
    for peer in range(peers):
        target = lax.rem(me[0] + peer, peers)
        for tile in range(tiles):
            lanes = slice(tile * LANES, (tile + 1) * LANES)
            for at in range(side_p):
                row = 8 * (tile * side_p + at)
                outs[peer][row : row + 8, :] = total[
                    pl.ds(pl.multiple_of(at * side_x + target * 8, 8), 8), lanes
                ]
            row = 8 * tiles * side_p + tile
            outs[peer][row : row + 1, :] = summed[:, lanes]


def join_kernel(peers, scale, beams_all, me, *refs):
    parts = refs[:peers]
    out, rows = refs[peers:]
    span, trials, beams = out.shape
    tiles = span * trials // LANES
    side_p = beams // 8 // peers
    base = 8 * tiles * side_p
    means = parts[0][base : base + tiles, :]
    for peer in range(1, peers):
        means = means + parts[peer][base : base + tiles, :]
    means = means * (1.0 / beams_all)
    for peer in range(peers):
        source = lax.rem(me[0] + peers - peer, peers)
        for tile in range(tiles):
            for at in range(side_p):
                row = 8 * (tile * side_p + at)
                value = (parts[peer][row : row + 8, :] - means[tile : tile + 1, :]) * scale
                for line in range(8):
                    rows[tile, pl.ds(line * side_p * peers + source * side_p + at, 1), :] = value[
                        line : line + 1, :
                    ]
    for tile in range(tiles):
        turned = rows[tile].T
        out[2 * tile] = turned[:trials]
        out[2 * tile + 1] = turned[trials:]


def fast_device(samples, fir_taps, beam_y, beam_x, delays):
    dishes, points = samples.shape
    taps_count, nfft = fir_taps.shape
    span = points // nfft
    side_x, side_y = beam_x.shape[1], beam_y.shape[1]
    trials, channels = delays.shape
    peers = lax.axis_size("chan")
    me = lax.axis_index("chan")
    side_p = side_y // peers
    pairs = side_p // PAIR
    groups = dishes // side_y // GROUP_X
    radix = nfft // LANES

    chunks = []
    top, size = span, 1
    while top > 0:
        size = 1 if top == 1 else min(size, top - 1)
        chunks.append((top - size, size))
        top, size = top - size, 2 * size

    tables, twist = dft_tables(nfft)
    mat_high = tables.astype(BF16)
    mat_low = (tables - mat_high.astype(np.float32)).astype(BF16)

    spot = me.reshape(1)
    count_tm = lax.axis_size("tm")
    forward = [(i, i + 1) for i in range(count_tm - 1)]
    bounds = sorted({low - taps_count + 1 for low, _ in chunks[1:]}, reverse=True)
    bounds = [bound for bound in bounds if bound < 0]
    bounds = bounds[:1] + bounds[-1:] if len(bounds) > 2 else bounds
    hists, hist_base, pieces = [], {}, []
    upper = 0
    for bound in bounds:
        for frame in range(bound, upper):
            hist_base[frame] = (len(pieces), frame - bound)
        first_low = chunks[0][0] - taps_count + 1
        pieces.append((span + bound - first_low, upper - bound))
        upper = bound
    total = None
    sent = []
    for at, (low_spec, specs) in enumerate(chunks):
        frames = range(low_spec - taps_count + 1, low_spec + specs)
        used = sorted({hist_base[f][0] for f in frames if f < 0})
        base = {f: (used.index(hist_base[f][0]), hist_base[f][1]) for f in frames if f < 0}
        outs = front(
            samples, [hists[i] for i in used], base, fir_taps, twist, mat_high, mat_low, beam_y, spot,
            low_spec, specs, peers, pairs, () if at else tuple(pieces),
        )
        order = sorted(range(1, peers), key=lambda r: abs(r - peers // 2))
        got = [outs[0]] + [None] * (peers - 1)
        for shift in order:
            got[shift] = lax.ppermute(
                outs[shift], "chan", [(i, (i + shift) % peers) for i in range(peers)]
            )
        sent.append((low_spec, got))
        if at == 0:
            for which in range(len(pieces)):
                hists.append(lax.ppermute(outs[peers + which], "tm", forward))
    delays, beam_x, sent[-1][1][0] = lax.optimization_barrier((delays, beam_x, sent[-1][1][0]))
    real, imag = beam_x[0], beam_x[1]
    blocks = jnp.stack([jnp.stack([real, -imag]), jnp.stack([imag, real])])
    blocks = blocks.reshape(2, 2, side_x, peers, groups, GROUP_X)[:, :, :, ::-1]
    blocks = jnp.concatenate([blocks, blocks], axis=3)
    blocks = lax.dynamic_slice_in_dim(blocks, peers - 1 - me, peers, 3)
    blocks = blocks.transpose(0, 2, 3, 4, 1, 5)[:, None, :, :, :, None, :, :]
    eye = jnp.asarray(np.eye(PAIR), BF16)[None, :, None, None, None, :, None, None]
    steer_x = (blocks * eye).reshape(2 * PAIR * side_x, peers * groups * PAIR * 2 * GROUP_X)

    by_bin = delays.reshape(trials, channels // radix, radix).transpose(2, 1, 0)
    folded = jnp.concatenate([by_bin[radix // 2 : radix // 2 + 1], by_bin[radix // 2 + 1 :][::-1, ::-1]])
    ordered = jnp.concatenate([by_bin[: radix // 2], folded], axis=1).reshape(channels, trials)
    ordered = jnp.concatenate([ordered, ordered], axis=1)

    for low_spec, got in sent:
        total = back(got, steer_x, ordered, total, low_spec, span, low_spec == 0)
    early, own = total

    came = lax.ppermute(early, "tm", [(i + 1, i) for i in range(count_tm - 1)])
    smem = pl.BlockSpec(memory_space=pltpu.SMEM)
    vmem = pl.BlockSpec(memory_space=pltpu.VMEM)
    tiles = span * trials // LANES
    rows = (8 * side_p + 1) * tiles
    dealt = pl.pallas_call(
        functools.partial(deal_kernel, peers),
        out_shape=[jax.ShapeDtypeStruct((rows, LANES), F32) for _ in range(peers)],
        in_specs=[smem, vmem, vmem],
        out_specs=[vmem] * peers,
        scratch_shapes=[pltpu.VMEM(own.shape, F32)],
        name="deal",
    )(spot, own, came)
    joined = [dealt[0]]
    joined += [None] * (peers - 1)
    for shift in order:
        joined[shift] = lax.ppermute(
            dealt[shift], "chan", [(i, (i + shift) % peers) for i in range(peers)]
        )
    series = pl.pallas_call(
        functools.partial(join_kernel, peers, 1.0 / math.sqrt(channels), side_x * side_y),
        out_shape=jax.ShapeDtypeStruct((span, trials, own.shape[0]), F32),
        in_specs=[smem] + [vmem] * peers,
        out_specs=vmem,
        scratch_shapes=[pltpu.VMEM((tiles, own.shape[0], LANES), F32)],
        name="join",
    )(spot, *joined)
    return series.transpose(2, 0, 1)


def on_device(samples, fir_taps, beam_y, beam_x, delays):
    dishes, points = samples.shape
    taps_count, nfft = fir_taps.shape
    side_x, side_y = beam_x.shape[1], beam_y.shape[1]
    trials, channels = delays.shape
    peers = lax.axis_size("chan")
    span = points // nfft
    fits = (
        dishes % (side_y * GROUP_X) == 0
        and side_y % (peers * PAIR) == 0
        and side_x == 8 * peers
        and 2 * trials == LANES
        and nfft % (4 * LANES) == 0
        and channels * 2 == nfft
        and span % 2 == 0
        and taps_count - 1 <= span
    )
    if fits:
        return fast_device(samples, fir_taps, beam_y, beam_x, delays)
    return plain_device(samples, fir_taps, beam_y, beam_x, delays)


def solution(mesh):
    return jax.shard_map(
        on_device,
        mesh=mesh,
        in_specs=(P("chan", "tm"), P(), P(), P(), P()),
        out_specs=P("chan", "tm", None),
        check_vma=False,
    )
```
